32 devices in a mesh: sec: 2 (over x), ep: 4 (over z), tp: 4 (over y, core).
Axes of the slice: x: 2, y: 2, z: 4, core: 2. Of those that a mesh axis runs over, the one named last changes fastest.
Arguments:
- queries: bfloat16 [32, 64, 576], P(('sec', 'ep'), 'tp')
- cache: bfloat16 [32, 32, 576], P(('sec', 'ep'))
- lengths: int32 [32], P(('sec', 'ep')), may hold values from 2 to 32, as said below
- w_uv: bfloat16 [64, 512, 128], P('tp'), may hold values from -0.25 to 0.25
- w_out: bfloat16 [8192, 7168], P('tp', 'ep'), may hold values from -0.0625 to 0.0625
- residual: bfloat16 [32, 7168], P(('sec', 'ep'), 'tp')
- gain: float32 [7168], P('tp'), may hold values from 0.5 to 1.5
- expert_ids: int32 [32, 4], P(('sec', 'ep')), may hold values from 0 to 15, all different within a row; in each aligned block of 4 rows (0 to 3, 4 to 7, ...) at most 2 rows name the same one
- expert_weights: float32 [32, 4], P(('sec', 'ep')), may hold values from 0.2 to 1
- w_gate: bfloat16 [128, 7168, 256], P(('sec', 'ep'), 'tp'), may hold values from -0.0625 to 0.0625
- w_up: bfloat16 [128, 7168, 256], P(('sec', 'ep'), 'tp'), may hold values from -0.0625 to 0.0625
- w_down: bfloat16 [128, 256, 7168], P(('sec', 'ep'), None, 'tp'), may hold values from -0.125 to 0.125
Outputs:
- next_state: bfloat16 [32, 7168], P(('sec', 'ep'), 'tp')
The draws below stay inside these ranges and needn't reach their ends.
Inputs may be any that keep to these rules, and one draw needn't show every extreme that they name: `expert_ids`: within each device's rows (aligned blocks of 4 requests) no expert is named by more than 2 routes, a bound that some block reaches. `lengths`: the first request of each aligned block of 4 requests has all 32 positions live.
All inputs are finite; a program needn't handle non-finite values.
Results may differ from the reference program's by a relative error of at most 0.0058.
Values may be sent and summed in bfloat16 or wider, within the bound.
No kernel may reach another device: no remote copies, remote signals or barrier semaphores. Data moves between devices by JAX's collectives and lax.ppermute only.
A program may use at most 128 MiB of HBM per device.

```python
import math
import jax
import jax.numpy as jnp
import numpy as np
from jax import lax

D = 7168
HEADS = 64
LATENT = 512
ROPE = 64
VDIM = 128
FF = 2048
HSPLIT = 8
HID = 256
EXPERTS = 16
TOPK = 4
REQ_DEV = 4
LEN = 32
CAP = 2
TOKENS = 32
N_SEC = 2
N_EP = 4


def latent_keys(key):
    return jax.random.normal(jax.random.fold_in(key, 101), (TOKENS, LEN, LATENT + ROPE), jnp.float32)


def draw_cache(key, part):
    base_draw = latent_keys(key)
    return base_draw.astype(jnp.bfloat16)


def draw_queries(key, part):
    normal_draw = jax.random.normal(jax.random.fold_in(key, 103), (TOKENS, HEADS, LATENT + ROPE), jnp.float32)
    return normal_draw.astype(jnp.bfloat16)


def draw_lengths(key, part):
    length_draw = jax.random.randint(jax.random.fold_in(key, 105), (TOKENS,), 2, LEN + 1, jnp.int32)
    leading = jnp.arange(TOKENS) % REQ_DEV == 0
    return jnp.where(leading, LEN, length_draw).astype(jnp.int32)


def draw_residual(key, part):
    row_scale = jnp.exp(jax.random.uniform(jax.random.fold_in(key, 106), (TOKENS, 1), jnp.float32, -1.204, 1.099))
    column_scale = jnp.exp(jax.random.uniform(jax.random.fold_in(key, 107), (1, D), jnp.float32, -1.204, 1.099))
    entries = jax.random.normal(jax.random.fold_in(key, 108), (TOKENS, D), jnp.float32)
    return (entries * row_scale * column_scale).astype(jnp.bfloat16)


def level_of(key, shape, pieces, smallest, largest):
    factor_of, own = 1.0, jax.random.fold_in(key, 6)
    for dim, blocks in pieces:
        heights = jnp.exp(jax.random.uniform(jax.random.fold_in(own, dim), (blocks,), jnp.float32, smallest / len(pieces), largest / len(pieces)))
        factor_of = factor_of * jnp.repeat(heights, shape[dim] // blocks).reshape([-1 if axis == dim else 1 for axis in range(len(shape))])
    return factor_of


def shared_out(rng, own, number, rows, count, top, most, lean):
    sequence = jax.random.permutation(rng, count)
    heavy_load, common = portions_of(count, rows * top, most, lean, True), portions_of(count, rows * top, most, lean, False)
    places = jnp.arange(count)

    def named(sizes, offset_by):
        used = int((sizes > 0).sum())
        fixed = max(1, used // 4)
        moved = fixed + (places - fixed + offset_by * (used - fixed)) % max(1, count - fixed)
        return jnp.zeros((count,), jnp.int32).at[sequence[jnp.where(places < fixed, places, moved)]].set(jnp.asarray(sizes, jnp.int32))

    sizes = jnp.where(number % 4 == 0, named(heavy_load, number // 4), named(common, number - number // 4 - 1))
    mixed = jax.random.permutation(jax.random.fold_in(own, 3), count)
    donor, taker = mixed[0:count // 2 * 2:2], mixed[1:count // 2 * 2:2]
    slack = jnp.minimum(sizes[donor] - 1, most - sizes[taker]) // 2
    slack = jnp.where((donor == sequence[0]) | (taker == sequence[0]) | (sizes[taker] == 0), 0, jnp.maximum(slack, 0))
    moved = jax.random.randint(jax.random.fold_in(own, 4), (count // 2,), 0, 1 << 20) % (slack + 1)
    sizes = sizes.at[donor].add(-moved).at[taker].add(moved)
    items = jnp.searchsorted(jnp.cumsum(sizes), jnp.arange(rows * top), side="right").astype(jnp.int32)
    table = items.reshape(top, rows).T
    table = table[jax.random.permutation(jax.random.fold_in(own, 1), rows)]
    offset_by = jax.random.randint(jax.random.fold_in(own, 2), (rows, 1), 0, top)
    return jnp.take_along_axis(table, (jnp.arange(top)[None, :] + offset_by) % top, axis=1)


def portions_of(number_of, total, reach, slope, full):
    loads = [(1 << 20) // math.isqrt(rank ** slope) + 1 for rank in range(1, number_of + 1)]
    largest = reach if full else min(reach, max(-(-total // number_of), total * loads[0] // sum(loads)))
    least = 1 if total - largest >= number_of - 1 else 0
    counts, spare = [largest] + [least] * (number_of - 1), total - largest - least * (number_of - 1)
    while spare > 0:
        candidates = [i for i in range(1, number_of) if counts[i] < largest] or [i for i in range(1, number_of) if counts[i] < reach]
        mass, left = sum([loads[i] for i in candidates]), spare
        for i in candidates:
            addition = min(reach - counts[i], max(1, left * loads[i] // mass), spare)
            counts[i] = counts[i] + addition
            spare = spare - addition
    return np.array(counts)


def scatter_about(key, extent, width, limit, split=(), kind=jnp.bfloat16):
    level = level_of(key, extent, split, -0.22, 0.18) if split else 1.0
    array = jax.random.normal(key, extent, jnp.float32) * width * level
    return jnp.minimum(jnp.maximum(array, -limit), limit).astype(kind)


def setup_inputs(seed: int = 0) -> dict:
    arg_keys = jax.random.split(jax.random.key(seed), 13)
    queries = draw_queries(jax.random.fold_in(arg_keys[12], 71), 0)
    cache = draw_cache(jax.random.fold_in(arg_keys[12], 71), 0)
    lengths = draw_lengths(jax.random.fold_in(arg_keys[12], 71), 0)
    w_uv = scatter_about(arg_keys[3], (HEADS, LATENT, VDIM), LATENT ** -0.5, 0.25, ((0, 4),))
    w_out = scatter_about(arg_keys[4], (HEADS * VDIM, D), (HEADS * VDIM) ** -0.5, 0.0625, ((0, 4), (1, 4)))
    residual = draw_residual(jax.random.fold_in(arg_keys[12], 71), 0)
    gain = jnp.clip(1.0 + 0.1 * jax.random.normal(arg_keys[6], (D,), jnp.float32), 0.5, 1.5)
    expert_ids_keys = jax.random.split(jax.random.fold_in(arg_keys[7], 1), TOKENS // REQ_DEV)
    expert_ids_turns = jax.random.permutation(jax.random.fold_in(arg_keys[7], 3), TOKENS // REQ_DEV)
    expert_ids = jax.vmap(lambda own, number: shared_out(jax.random.fold_in(arg_keys[7], 2), own, number, REQ_DEV, EXPERTS, TOPK, CAP, 2))(expert_ids_keys, expert_ids_turns).reshape((TOKENS, TOPK))
    expert_weights = jnp.clip(jnp.exp(math.log(1.0) - 1.609438 * jax.random.uniform(arg_keys[8], (TOKENS, TOPK), jnp.float32) ** level_of(arg_keys[8], (TOKENS, TOPK), ((0, 8),), -0.2, 0.2)), 0.2, 1.0)
    w_gate = scatter_about(arg_keys[9], (EXPERTS * HSPLIT, D, HID), D ** -0.5, 0.0625, ((0, 8), (1, 4)))
    w_up = scatter_about(arg_keys[10], (EXPERTS * HSPLIT, D, HID), D ** -0.5, 0.0625, ((0, 8), (1, 4)))
    w_down = scatter_about(arg_keys[11], (EXPERTS * HSPLIT, HID, D), FF ** -0.5, 0.125, ((0, 8), (2, 4)))
    return {"queries": queries, "cache": cache, "lengths": lengths, "w_uv": w_uv, "w_out": w_out, "residual": residual, "gain": gain, "expert_ids": expert_ids, "expert_weights": expert_weights, "w_gate": w_gate, "w_up": w_up, "w_down": w_down}


score_scale = 0.07216878364870322
norm_eps = 1e-06

def reference(queries, cache, lengths, w_uv, w_out, residual, gain, expert_ids, expert_weights, w_gate, w_up, w_down):
    scores = jnp.einsum('thc,tlc->thl', queries.astype(jnp.float32), cache.astype(jnp.float32)) * score_scale
    positions = jnp.arange(LEN, dtype=jnp.int32)
    live_mask = positions[None, None, :] < lengths[:, None, None]
    scores = jnp.where(live_mask, scores, -1e+30)
    row_top = lax.optimization_barrier(jnp.max(scores, axis=-1, keepdims=True))
    raw_weights = jnp.where(live_mask, jnp.exp(scores - row_top), 0.0)
    probs = (raw_weights / lax.optimization_barrier(jnp.sum(raw_weights, axis=-1, keepdims=True))).astype(jnp.bfloat16)
    latent = jnp.einsum('thl,tlc->thc', probs.astype(jnp.float32), cache[:, :, :LATENT].astype(jnp.float32)).astype(jnp.bfloat16)
    values = jnp.einsum('thc,hcv->thv', latent.astype(jnp.float32), w_uv.astype(jnp.float32)).astype(jnp.bfloat16)
    values = values.reshape(TOKENS, HEADS * VDIM)
    attention = jnp.dot(values, w_out, preferred_element_type=jnp.float32)
    hidden_state = (residual.astype(jnp.float32) + attention).astype(jnp.bfloat16)
    flat_ids = expert_ids.reshape(-1).astype(jnp.int32)
    route_count = TOKENS * TOPK
    token_of = (jnp.arange(route_count, dtype=jnp.int32) // TOPK).astype(jnp.int32)
    onehot = (flat_ids[:, None] == jnp.arange(EXPERTS, dtype=jnp.int32)[None, :]).astype(jnp.int32)
    rank = lax.optimization_barrier(jnp.sum((jnp.cumsum(onehot, axis=0) - onehot) * onehot, axis=1)).astype(jnp.int32)
    room = N_SEC * N_EP * CAP
    route_rows = hidden_state[token_of]

    def one_expert(expert):
        mine = flat_ids == expert
        where_to = jnp.where(mine, rank, room).astype(jnp.int32)
        buffer_rows = jnp.zeros((room, D), jnp.bfloat16).at[where_to].set(route_rows, mode='drop')
        buffer_wide = buffer_rows.astype(jnp.float32)
        inv_rms = lax.rsqrt(lax.optimization_barrier(jnp.sum(buffer_wide * buffer_wide, axis=-1)) / D + norm_eps)
        scaled = (buffer_wide * gain[None, :]).astype(jnp.bfloat16)

        def piece_step(running, piece_index):
            piece_row = (expert * HSPLIT + piece_index).astype(jnp.int32)
            gate_block = lax.dynamic_index_in_dim(w_gate, piece_row, 0, keepdims=False)
            up_block = lax.dynamic_index_in_dim(w_up, piece_row, 0, keepdims=False)
            down_block = lax.dynamic_index_in_dim(w_down, piece_row, 0, keepdims=False)
            gate_part = jnp.dot(scaled, gate_block, preferred_element_type=jnp.float32) * inv_rms[:, None]
            up_part = jnp.dot(scaled, up_block, preferred_element_type=jnp.float32) * inv_rms[:, None]
            activated = (jax.nn.silu(gate_part) * up_part).astype(jnp.bfloat16)
            piece_out = jnp.dot(activated, down_block, preferred_element_type=jnp.float32).astype(jnp.bfloat16)
            return (running + piece_out.astype(jnp.float32), None)
        summed, unused = lax.scan(piece_step, jnp.zeros((room, D), jnp.float32), jnp.arange(HSPLIT, dtype=jnp.int32))
        return summed
    expert_outs = lax.map(one_expert, jnp.arange(EXPERTS, dtype=jnp.int32))
    route_out = expert_outs[flat_ids, rank]
    mixture = lax.optimization_barrier(jnp.sum(route_out.reshape(TOKENS, TOPK, D) * expert_weights[:, :, None], axis=1))
    return (hidden_state.astype(jnp.float32) + mixture).astype(jnp.bfloat16)
```

```python
import jax
import jax.numpy as jnp
from jax import lax
from jax.experimental import pallas as pl
from jax.experimental.pallas import tpu as pltpu
from jax.sharding import PartitionSpec as P

D = 7168
HSPLIT = 8
EXPERTS = 16
CAP = 2


score_scale = 0.07216878364870322
norm_eps = 1e-06

f32 = jnp.float32
bf16 = jnp.bfloat16
VMEM = pl.BlockSpec(memory_space=pltpu.VMEM)
SMEM = pl.BlockSpec(memory_space=pltpu.SMEM)


def cost(micros):
    return pl.CostEstimate(flops=micros * 1_000_000_000, bytes_accessed=1_000_000, transcendentals=0)


COST0, COST1, COST2 = cost(10), cost(30), cost(60)


def call(body, outs, args, specs, scratch=(), limit=4 << 20, cost=None):
    return pl.pallas_call(
        body,
        out_shape=[jax.ShapeDtypeStruct(s, d) for s, d in outs],
        in_specs=specs,
        out_specs=[VMEM] * len(outs),
        scratch_shapes=list(scratch),
        compiler_params=pltpu.CompilerParams(vmem_limit_bytes=limit),
        cost_estimate=cost,
    )(*args)


def dot(a, b):
    return jnp.dot(a, b, preferred_element_type=f32)


def onehot(shape, want):
    row = lax.broadcasted_iota(jnp.int32, shape, 0)
    col = lax.broadcasted_iota(jnp.int32, shape, 1)
    return want(row, col).astype(f32).astype(bf16)


def attend_body(picks, lengths, queries, cache, w_uv, out, wide):
    rows, heads, _ = queries.shape
    latent_width = w_uv.shape[1]
    vdim = w_uv.shape[2]
    for r in range(rows):
        keys = cache[r]
        scores = (
            lax.dot_general(queries[r], keys, (((1,), (1,)), ((), ())), preferred_element_type=f32)
            * score_scale
        )
        live = lax.broadcasted_iota(jnp.int32, scores.shape, 1) < lengths[r]
        scores = jnp.where(live, scores, -1e30)
        top = jnp.max(scores, axis=-1, keepdims=True)
        raw = jnp.where(live, jnp.exp(scores - top), 0.0)
        probs = (raw / jnp.sum(raw, axis=-1, keepdims=True)).astype(bf16)
        wide[r] = dot(probs, keys[:, :latent_width])
    copies = out.shape[0]
    per = out.shape[2] // vdim
    for h in range(heads):
        value = dot(wide[:, h, :].astype(bf16), w_uv[h]).astype(bf16)
        piece, lane = h // per, (h % per) * vdim
        for e in range(copies):
            out[e, piece * rows : (piece + 1) * rows, lane : lane + vdim] = value


def plan_body(picks):
    core = lax.axis_index("tp") % 2
    _, lines, packed_lines = picks.shape
    ep = lax.axis_size("ep")
    rows = lines // ep
    for half in range(2):

        def want(row, col):
            block = row // rows
            parity = jnp.where(block < ep // 2, core, 1 - core)
            source = 2 * (block % (ep // 2)) + parity
            return col == source * 2 * rows + half * rows + row % rows

        picks[half] = onehot((lines, packed_lines), want)


def project_body(values, picks, w_out, keep, send):
    ep, packed, width = values.shape
    rows = packed // 2
    flat = values[...].reshape(ep * packed, width)
    total = None
    for half in range(2):
        picked = dot(picks[half], flat).astype(bf16)
        part = dot(picked, w_out[half * width : (half + 1) * width, :])
        total = part if total is None else total + part
    for i in range(ep // 2):
        keep[i] = total[i * rows : (i + 1) * rows]
        send[i] = total[(i + ep // 2) * rows : (i + ep // 2 + 1) * rows]


def pair_body(keep, got, first, second):
    y = lax.axis_index("tp") // 2
    first[...] = keep[y] + got[y]
    second[...] = keep[1 - y] + got[1 - y]


def route_body(ids, weights, place, mix):
    rows, top = ids.shape
    slots = []
    for r in range(rows):
        for k in range(top):
            expert = ids[r, k]
            rank = jnp.int32(0)
            for q in range(r):
                for j in range(top):
                    rank = rank + (ids[q, j] == expert).astype(jnp.int32)
            slots.append((r, k, expert * CAP + rank))
    packed = place.shape[1]
    per = packed // 2
    row = lax.broadcasted_iota(jnp.int32, place.shape, 0)
    col = lax.broadcasted_iota(jnp.int32, place.shape, 1)
    slot = (row // packed) * per + row % per
    half = (row % packed) // per
    acc = jnp.zeros(place.shape, f32)
    for r, k, where in slots:
        acc = acc + jnp.where((slot == where) & (col == half * rows + r), 1.0, 0.0)
    place[...] = acc.astype(bf16)
    row = lax.broadcasted_iota(jnp.int32, mix.shape, 0)
    col = lax.broadcasted_iota(jnp.int32, mix.shape, 1)
    slot = (col // packed) * per + col % per
    half = (col % packed) // per
    acc = jnp.zeros(mix.shape, f32)
    for r, k, where in slots:
        acc = acc + jnp.where(
            (slot == where) & (row // (3 * rows) == half) & (row % rows == r), weights[r, k], 0.0
        )
    high = acc.astype(bf16)
    left = acc - high.astype(f32)
    middle = left.astype(bf16)
    low = (left - middle.astype(f32)).astype(bf16)
    part = (row // rows) % 3
    mix[...] = jnp.where(
        part == 0, high.astype(f32), jnp.where(part == 1, middle.astype(f32), low.astype(f32))
    ).astype(bf16)


def spread_body(residual, first, second, place, gain, state, sending, gain_out):
    gain_out[...] = gain[...]
    new = (residual[...].astype(f32) + (first[...] + second[...])).astype(bf16)
    state[...] = new
    width = new.shape[1] // 2
    wide = new.astype(f32)
    halves = jnp.concatenate([wide[:, :width], wide[:, width:]], axis=0).astype(bf16)
    table = dot(place[...], halves).astype(bf16)
    sending[...] = table.reshape(sending.shape)


def pick_rows(arrived, expert):
    groups, packed, width = arrived.shape
    per = packed // 2
    flat = arrived[...].reshape(groups * packed, width)
    out = []
    for half in range(2):
        want = lambda row, col: (
            col == (row // CAP) * packed + half * per + expert * CAP + row % CAP
        )
        out.append(dot(onehot((groups * CAP, groups * packed), want), flat))
    return jnp.concatenate(out, axis=1)


def expert_partial(arrived, gain, w_gate, w_up, expert, store):
    rows = pick_rows(arrived, expert)
    square = jnp.sum(rows * rows, axis=1, keepdims=True)
    scaled = (rows * gain[...]).astype(bf16)
    hid = w_gate.shape[2]
    for p in range(HSPLIT):
        at = expert * HSPLIT + p
        store(p * hid, dot(scaled, w_gate[at]))
        store((HSPLIT + p) * hid, dot(scaled, w_up[at]))
    high = square.astype(bf16).astype(f32)
    middle = (square - high).astype(bf16).astype(f32)
    low = square - high - middle
    lane = lax.broadcasted_iota(jnp.int32, (rows.shape[0], 128), 1)
    store(
        2 * HSPLIT * hid,
        jnp.where(
            lane == 0,
            high,
            jnp.where(lane == 1, middle, jnp.where(lane == 2, low, 0.0)),
        ),
    )


def experts_away_body(arrived, gain, w_gate, w_up, out):
    core = lax.axis_index("tp") % 2

    def store(lane, value):
        out[:, lane : lane + value.shape[1]] = value.astype(bf16)

    expert_partial(arrived, gain, w_gate, w_up, 1 - core, store)


def experts_own_body(arrived, gain, w_gate, w_up, out):
    core = lax.axis_index("tp") % 2

    def store(lane, value):
        out[:, lane : lane + value.shape[1]] = value

    expert_partial(arrived, gain, w_gate, w_up, core, store)


def merge_body(own, got, total, send):
    whole = own[...] + got[...].astype(f32)
    total[...] = whole
    tail = whole.shape[1] - 128
    send[:, :tail] = whole[:, :tail].astype(bf16)
    square = jnp.sum(whole[:, tail:], axis=1, keepdims=True)
    high = square.astype(bf16).astype(f32)
    middle = (square - high).astype(bf16).astype(f32)
    low = square - high - middle
    lane = lax.broadcasted_iota(jnp.int32, (whole.shape[0], 128), 1)
    send[:, tail:] = jnp.where(
        lane == 0,
        high,
        jnp.where(lane == 1, middle, jnp.where(lane == 2, low, 0.0)),
    ).astype(bf16)


def act_body(total, got, out):
    hidden = out.shape[1]
    whole = total[...] + got[...].astype(f32)
    square = jnp.sum(whole[:, 2 * hidden :], axis=1, keepdims=True)
    inv_rms = lax.rsqrt(square / D + norm_eps)
    gate = whole[:, :hidden] * inv_rms
    up = whole[:, hidden : 2 * hidden] * inv_rms
    out[...] = (gate / (1.0 + jnp.exp(-gate)) * up).astype(bf16)


def down_one(act, w_down, expert):
    hid = w_down.shape[1]
    total = None
    for p in range(HSPLIT):
        part = dot(act[:, p * hid : (p + 1) * hid], w_down[expert * HSPLIT + p])
        total = part if total is None else total + part
    return total.astype(bf16)


def down_body(act, act_away, w_down, out):
    core = lax.axis_index("tp") % 2
    groups, packed, width = out.shape
    per = packed // 2
    table = None
    for expert, source in ((core, act), (1 - core, act_away)):
        block = down_one(source, w_down, expert)
        for half in range(2):
            want = lambda row, col: (
                row == (col // CAP) * packed + half * per + expert * CAP + col % CAP
            )
            part = dot(
                onehot((groups * packed, groups * CAP), want),
                block[:, half * width : (half + 1) * width],
            )
            table = part if table is None else table + part
    out[...] = table.astype(bf16).reshape(out.shape)


def finish_body(state, back, mix, out):
    groups, packed, width = back.shape
    rows = state.shape[0]
    mixed = dot(mix[...], back[...].reshape(groups * packed, width))
    for half in range(2):
        base = half * 3 * rows
        add = (
            mixed[base : base + rows]
            + mixed[base + rows : base + 2 * rows]
            + mixed[base + 2 * rows : base + 3 * rows]
        )
        lanes = slice(half * width, (half + 1) * width)
        out[:, lanes] = (state[:, lanes].astype(f32) + add).astype(bf16)


def local(
    queries,
    cache,
    lengths,
    w_uv,
    w_out,
    residual,
    gain,
    expert_ids,
    expert_weights,
    w_gate,
    w_up,
    w_down,
):
    sec, ep, tp = (lax.axis_size(a) for a in ("sec", "ep", "tp"))
    rows, heads, _ = queries.shape
    columns = residual.shape[1]
    vdim = w_uv.shape[2]
    groups = sec * ep
    slots = EXPERTS // groups * CAP
    half = columns // 2
    hidden = HSPLIT * w_gate.shape[2]
    lines = groups * CAP
    swap_core = [(t, t ^ 1) for t in range(tp)]
    swap_chip = [(t, t ^ 2) for t in range(tp)]

    place, mix = call(
        route_body,
        [((groups * 2 * slots, 2 * rows), bf16), ((6 * rows, groups * 2 * slots), bf16)],
        (expert_ids, expert_weights),
        [SMEM, SMEM],
    )
    (picks,) = call(
        plan_body, [((2, ep * rows, 2 * ep * rows), bf16)], (), [], cost=COST0
    )
    (values,) = call(
        attend_body,
        [((ep, 2 * rows, heads * vdim // 2), bf16)],
        (picks, lengths, queries, cache, w_uv),
        [VMEM, SMEM, VMEM, VMEM, VMEM],
        [pltpu.VMEM((rows, heads, w_uv.shape[1]), f32)],
        cost=COST1,
    )
    values = lax.all_to_all(values, "ep", split_axis=0, concat_axis=0, tiled=True)
    keep, send = call(
        project_body,
        [((ep // 2, rows, columns), f32)] * 2,
        (values, picks, w_out),
        [VMEM, VMEM, VMEM],
        cost=COST2,
    )
    got = lax.ppermute(send, "tp", swap_core)
    first, second = call(
        pair_body, [((rows, columns), f32)] * 2, (keep, got), [VMEM, VMEM]
    )

    def turn(flip):
        pairs = []
        for s in range(sec):
            for e in range(ep):
                for t in range(tp):
                    to = (s * ep + t % 2 + 2 * ((t // 2) ^ flip)) * tp + e
                    pairs.append(((s * ep + e) * tp + t, to))
        return pairs

    axes = ("sec", "ep", "tp")
    first = lax.ppermute(first, axes, turn(0))
    second = lax.ppermute(second, axes, turn(1))
    state, sending, gain = call(
        spread_body,
        [((rows, columns), bf16), ((groups, 2 * slots, half), bf16), ((1, columns), f32)],
        (residual, first, second, place, gain.reshape(1, columns)),
        [VMEM] * 5,
        cost=cost(20),
    )
    arrived = lax.all_to_all(sending, ("sec", "ep"), split_axis=0, concat_axis=0, tiled=True)
    wide = 2 * hidden + 128
    (away,) = call(
        experts_away_body,
        [((lines, wide), bf16)],
        (arrived, gain, w_gate, w_up),
        [VMEM] * 4,
        cost=cost(20),
    )
    away = lax.ppermute(away, "tp", swap_core)
    (own,) = call(
        experts_own_body,
        [((lines, wide), f32)],
        (arrived, gain, w_gate, w_up),
        [VMEM] * 4,
        cost=cost(20),
    )
    total, send = call(
        merge_body, [((lines, wide), f32), ((lines, wide), bf16)], (own, away), [VMEM] * 2
    )
    got = lax.ppermute(send, "tp", swap_chip)
    (act,) = call(act_body, [((lines, hidden), bf16)], (total, got), [VMEM] * 2)
    act_away = lax.ppermute(act, "tp", swap_core)
    (back,) = call(
        down_body,
        [((groups, 2 * slots, half), bf16)],
        (act, act_away, w_down),
        [VMEM] * 3,
    )
    back = lax.all_to_all(back, ("sec", "ep"), split_axis=0, concat_axis=0, tiled=True)
    (out,) = call(finish_body, [((rows, columns), bf16)], (state, back, mix), [VMEM] * 3)
    return out


def local_any(
    queries,
    cache,
    lengths,
    w_uv,
    w_out,
    residual,
    gain,
    expert_ids,
    expert_weights,
    w_gate,
    w_up,
    w_down,
):
    req_rows = queries.shape[0]
    latent_width = w_uv.shape[1]
    scores = (
        jnp.einsum("rhc,rlc->rhl", queries, cache, preferred_element_type=jnp.float32) * score_scale
    )
    positions = lax.broadcasted_iota(jnp.int32, scores.shape, 2)
    live_mask = positions < lengths[:, None, None]
    scores = jnp.where(live_mask, scores, -1e30)
    row_top = jnp.max(scores, axis=-1, keepdims=True)
    raw_weights = jnp.where(live_mask, jnp.exp(scores - row_top), 0.0)
    probs = (raw_weights / jnp.sum(raw_weights, axis=-1, keepdims=True)).astype(jnp.bfloat16)
    latent = jnp.einsum(
        "rhl,rlc->rhc", probs, cache[:, :, :latent_width], preferred_element_type=jnp.float32
    ).astype(jnp.bfloat16)
    values = jnp.einsum("rhc,hcv->rhv", latent, w_uv, preferred_element_type=jnp.float32).astype(
        jnp.bfloat16
    )
    values = values.reshape(req_rows, -1)
    projected = jnp.dot(
        lax.all_gather(values, "ep", axis=0, tiled=True), w_out, preferred_element_type=jnp.float32
    )
    full_rows = lax.all_to_all(projected, "ep", split_axis=0, concat_axis=1, tiled=True)
    attention = lax.psum_scatter(full_rows, "tp", scatter_dimension=1, tiled=True)
    hidden_state = (residual.astype(jnp.float32) + attention).astype(jnp.bfloat16)
    column_count = hidden_state.shape[1]
    topk_count = expert_ids.shape[1]
    flat_ids = expert_ids.reshape(-1)
    onehot = (flat_ids[:, None] == jnp.arange(EXPERTS, dtype=jnp.int32)[None, :]).astype(jnp.int32)
    rank = jnp.sum((jnp.cumsum(onehot, axis=0) - onehot) * onehot, axis=1)
    slot_index = flat_ids * CAP + rank
    route_rows = jnp.repeat(hidden_state, topk_count, axis=0)
    slot_table = (
        jnp.zeros((EXPERTS * CAP, column_count), jnp.bfloat16).at[slot_index].set(route_rows)
    )
    sending = jnp.repeat(slot_table.reshape(EXPERTS, CAP, column_count), HSPLIT, axis=0)
    sec_count = lax.axis_size("sec")
    ep_count = lax.axis_size("ep")
    groups = sec_count * ep_count
    local_pieces = w_gate.shape[0]
    sending = sending.reshape(groups, local_pieces * CAP, column_count)
    received = lax.all_to_all(sending, ("sec", "ep"), split_axis=0, concat_axis=0, tiled=True)
    arrived = received.reshape(groups, local_pieces, CAP, column_count)
    arrived_wide = arrived.astype(jnp.float32)
    squares = jnp.sum(arrived_wide * arrived_wide, axis=-1)
    scaled = (arrived_wide * gain[None, None, None, :]).astype(jnp.bfloat16)
    gate_part = jnp.einsum("gpcd,pdh->gpch", scaled, w_gate, preferred_element_type=jnp.float32)
    up_part = jnp.einsum("gpcd,pdh->gpch", scaled, w_up, preferred_element_type=jnp.float32)
    gate_part, up_part, squares = lax.psum((gate_part, up_part, squares), "tp")
    inv_rms = lax.rsqrt(squares / D + norm_eps)[..., None]
    activated = (jax.nn.silu(gate_part * inv_rms) * (up_part * inv_rms)).astype(jnp.bfloat16)
    piece_out = jnp.einsum(
        "gpch,phd->gpcd", activated, w_down, preferred_element_type=jnp.float32
    ).astype(jnp.bfloat16)
    returned = lax.all_to_all(
        piece_out.reshape(groups, local_pieces * CAP, column_count),
        ("sec", "ep"),
        split_axis=0,
        concat_axis=0,
        tiled=True,
    )
    per_expert = jnp.sum(
        returned.reshape(EXPERTS, HSPLIT, CAP, column_count).astype(jnp.float32), axis=1
    )
    route_out = per_expert.reshape(EXPERTS * CAP, column_count)[slot_index]
    mixture = jnp.sum(
        route_out.reshape(req_rows, topk_count, column_count) * expert_weights[:, :, None], axis=1
    )
    return (hidden_state.astype(jnp.float32) + mixture).astype(jnp.bfloat16)


def solution(mesh):
    in_specs = (
        P(("sec", "ep"), "tp", None),
        P(("sec", "ep"), None, None),
        P(("sec", "ep")),
        P("tp", None, None),
        P("tp", "ep"),
        P(("sec", "ep"), "tp"),
        P("tp"),
        P(("sec", "ep"), None),
        P(("sec", "ep"), None),
        P(("sec", "ep"), "tp", None),
        P(("sec", "ep"), "tp", None),
        P(("sec", "ep"), None, "tp"),
    )
    out_specs = P(("sec", "ep"), "tp")
    shape = mesh.shape
    small = shape["ep"] == 4 and shape["tp"] == 4 and shape["sec"] == 2
    body = local if small else local_any
    return jax.shard_map(body, mesh=mesh, in_specs=in_specs, out_specs=out_specs, check_vma=False)
```

```python
import jax
import jax.numpy as jnp
from jax import lax
from jax.experimental import pallas as pl
from jax.experimental.pallas import tpu as pltpu
from jax.sharding import PartitionSpec as P

D = 7168
HSPLIT = 8
EXPERTS = 16
CAP = 2


score_scale = 0.07216878364870322
norm_eps = 1e-06

f32 = jnp.float32
bf16 = jnp.bfloat16
VMEM = pl.BlockSpec(memory_space=pltpu.VMEM)
SMEM = pl.BlockSpec(memory_space=pltpu.SMEM)


def cost(micros):
    return pl.CostEstimate(flops=micros * 1_000_000_000, bytes_accessed=1_000_000, transcendentals=0)


COSTS = [cost(m) for m in (20, 1, 20, 60, 1, 1, 20, 20)]


def call(body, outs, args, specs, scratch=(), limit=4 << 20, cost=None):
    return pl.pallas_call(
        body,
        out_shape=[jax.ShapeDtypeStruct(s, d) for s, d in outs],
        in_specs=specs,
        out_specs=[VMEM] * len(outs),
        scratch_shapes=list(scratch),
        compiler_params=pltpu.CompilerParams(vmem_limit_bytes=limit),
        cost_estimate=cost,
    )(*args)


def dot(a, b):
    return jnp.dot(a, b, preferred_element_type=f32)


def onehot(shape, want):
    row = lax.broadcasted_iota(jnp.int32, shape, 0)
    col = lax.broadcasted_iota(jnp.int32, shape, 1)
    return want(row, col).astype(f32).astype(bf16)


def start_body(pick):
    me = lax.axis_index("ep")
    lines = pick.shape[0]
    block = lines // 4
    rows = block // 4

    def want(row, col):
        kind, e, r = row // block, (row % block) // rows, row % rows
        return col == (e ^ me) * block + kind * rows + r

    pick[...] = onehot(pick.shape, want)


def latent_body(lengths, queries, cache, pick, latent):
    rows, heads, _ = queries.shape
    width = latent.shape[2]
    scores = jnp.concatenate(
        [
            lax.dot_general(
                queries[r], cache[r], (((1,), (1,)), ((), ())), preferred_element_type=f32
            )
            for r in range(rows)
        ],
        axis=0,
    )
    owner = lax.broadcasted_iota(jnp.int32, scores.shape, 0) // heads
    limit = jnp.full(scores.shape, lengths[0], jnp.int32)
    for r in range(1, rows):
        limit = jnp.where(owner == r, lengths[r], limit)
    live = lax.broadcasted_iota(jnp.int32, scores.shape, 1) < limit
    scores = jnp.where(live, scores * score_scale, -1e30)
    top = jnp.max(scores, axis=-1, keepdims=True)
    raw = jnp.where(live, jnp.exp(scores - top), 0.0)
    probs = (raw / jnp.sum(raw, axis=-1, keepdims=True)).astype(bf16)
    for r in range(rows):
        latent[r] = dot(probs[r * heads : (r + 1) * heads], cache[r, :, :width])


def values_body(ids, latent, w_uv, residual, out):
    rows, heads, _ = latent.shape
    per = heads // 2
    halves = []
    for piece in range(2):
        parts = [
            dot(latent[:, h, :].astype(bf16), w_uv[h]) for h in range(piece * per, (piece + 1) * per)
        ]
        halves.append(jnp.concatenate(parts, axis=1))
    packed = 2 * rows
    out[:packed] = jnp.concatenate(halves, axis=0).astype(bf16)
    span = residual.shape[1] // 2
    wide = residual[...].astype(f32)
    row = lax.broadcasted_iota(jnp.int32, (rows, 128), 0)
    lane = lax.broadcasted_iota(jnp.int32, (rows, 128), 1)
    named = jnp.zeros((rows, 128), f32)
    for r in range(rows):
        for k in range(ids.shape[1]):
            named = jnp.where((row == r) & (lane == k), ids[r, k].astype(f32), named)
    halves = [
        jnp.concatenate([wide[:, h * span : (h + 1) * span], named], axis=1) for h in range(2)
    ]
    out[packed:] = jnp.concatenate(halves, axis=0).astype(bf16)


def project_body(pick, own, got1, got2, got3, w_out, out, extra):
    packed = own.shape[0] // 2
    flat = jnp.concatenate([ref[...] for ref in (own, got1, got2, got3)], axis=0)
    block, width = out.shape[0], own.shape[1]
    table = dot(pick[...], flat).astype(bf16)
    out[...] = dot(table[:block], w_out[:width]) + dot(table[block : 2 * block], w_out[width:])
    extra[...] = table[2 * block :]


def add_body(one, two, out):
    out[...] = (one[...].astype(f32) + two[...].astype(f32)).astype(bf16)


def choose_body(extra, got, known, choice):
    me, sec = lax.axis_index("ep"), lax.axis_index("sec")
    block = extra.shape[0] // 2
    rows = block // 4
    tokens = 2 * block
    span = known.shape[1] // 2
    first = jnp.concatenate([extra[:block], got[:block]], axis=0)
    second = jnp.concatenate([extra[block:], got[block:]], axis=0)
    known[:, :span] = first[:, :span].astype(f32)
    known[:, span:] = second[:, :span].astype(f32)
    ids = first[:, span:].astype(f32)
    lane = lax.broadcasted_iota(jnp.int32, ids.shape, 1)
    hits = jnp.zeros(ids.shape, f32)
    local_experts = EXPERTS // (2 * 4)
    for x in range(local_experts):
        expert = ((sec * 4 + me) * local_experts + x).astype(f32)
        found = jnp.sum(jnp.where((lane < 4) & (ids == expert), 1.0, 0.0), axis=1, keepdims=True)
        hits = hits + jnp.where(lane == x, found, 0.0)
    hits = hits.astype(bf16)
    across = lax.dot_general(
        onehot((8, 128), lambda row, col: row == col),
        hits,
        (((1,), (1,)), ((), ())),
        preferred_element_type=f32,
    )
    earlier = dot(
        across.astype(bf16),
        onehot((tokens, tokens), lambda row, col: (row // rows == col // rows) & (row < col)),
    )
    slots = 2 * 4 * CAP
    row = lax.broadcasted_iota(jnp.int32, (slots, tokens), 0)
    col = lax.broadcasted_iota(jnp.int32, (slots, tokens), 1)
    group, rank = row // CAP, (row % CAP).astype(f32)
    same = (group % 4 == (col % block) // rows) & ((group // 4) ^ sec == col // block)
    for x in range(local_experts):
        hit = jnp.broadcast_to(across[x : x + 1], (slots, tokens))
        before = jnp.broadcast_to(earlier[x : x + 1], (slots, tokens))
        choice[x * slots : (x + 1) * slots] = jnp.where(
            same & (hit > 0.5) & (before == rank), 1.0, 0.0
        ).astype(bf16)
    choice[local_experts * slots :] = onehot(
        (8, tokens), lambda row, col: (row < rows) & (col == me * rows + row)
    )


def mix_body(ids, weights, mix):
    rows, top = ids.shape
    slots = []
    for r in range(rows):
        for k in range(top):
            expert = ids[r, k]
            rank = jnp.int32(0)
            for q in range(r):
                for j in range(top):
                    rank = rank + (ids[q, j] == expert).astype(jnp.int32)
            slots.append((r, k, expert * CAP + rank))
    packed = 8
    per = packed // 2
    row = lax.broadcasted_iota(jnp.int32, mix.shape, 0)
    col = lax.broadcasted_iota(jnp.int32, mix.shape, 1)
    slot = (col // packed) * per + col % per
    half = (col % packed) // per
    acc = jnp.zeros(mix.shape, f32)
    for r, k, where in slots:
        acc = acc + jnp.where(
            (slot == where) & (row // (3 * rows) == half) & (row % rows == r), weights[r, k], 0.0
        )
    high = acc.astype(bf16)
    left = acc - high.astype(f32)
    middle = left.astype(bf16)
    low = (left - middle.astype(f32)).astype(bf16)
    part = (row // rows) % 3
    mix[...] = jnp.where(
        part == 0, high.astype(f32), jnp.where(part == 1, middle.astype(f32), low.astype(f32))
    ).astype(bf16)


def expert_partial(rows, gain, w_gate, w_up, expert, store):
    square = jnp.sum(rows * rows, axis=1, keepdims=True)
    scaled = (rows * gain[...]).astype(bf16)
    hid = w_gate.shape[2]
    for p in range(HSPLIT):
        at = expert * HSPLIT + p
        store(p * hid, dot(scaled, w_gate[at]))
        store((HSPLIT + p) * hid, dot(scaled, w_up[at]))
    high = square.astype(bf16).astype(f32)
    middle = (square - high).astype(bf16).astype(f32)
    low = square - high - middle
    lane = lax.broadcasted_iota(jnp.int32, (rows.shape[0], 128), 1)
    store(
        2 * HSPLIT * hid,
        jnp.where(
            lane == 0,
            high,
            jnp.where(lane == 1, middle, jnp.where(lane == 2, low, 0.0)),
        ),
    )


def experts_away_body(known, same, other, choice, gain, w_gate, w_up, out, mine, state):
    core = lax.axis_index("tp") % 2
    block = same.shape[0]
    lines = out.shape[0]
    hidden = jnp.concatenate(
        [
            (known[:block] + same[...].astype(f32)).astype(bf16),
            (known[block:] + other[...].astype(f32)).astype(bf16),
        ],
        axis=0,
    )
    table = dot(choice[...], hidden)
    first, second = table[:lines], table[lines : 2 * lines]
    mine[...] = jnp.where(core == 0, first, second).astype(bf16)
    state[...] = table[2 * lines : 2 * lines + state.shape[0]].astype(bf16)

    def store(lane, value):
        out[:, lane : lane + value.shape[1]] = value

    rows = jnp.where(core == 0, second, first)
    expert_partial(rows, gain, w_gate, w_up, 1 - core, store)


def experts_own_body(mine, gain, w_gate, w_up, out):
    core = lax.axis_index("tp") % 2

    def store(lane, value):
        out[:, lane : lane + value.shape[1]] = value

    expert_partial(mine[...].astype(f32), gain, w_gate, w_up, core, store)


def merge_body(own, got, total, send):
    whole = own[...] + got[...]
    total[...] = whole
    tail = whole.shape[1] - 128
    send[:, :tail] = whole[:, :tail].astype(bf16)
    square = jnp.sum(whole[:, tail:], axis=1, keepdims=True)
    high = square.astype(bf16).astype(f32)
    middle = (square - high).astype(bf16).astype(f32)
    low = square - high - middle
    lane = lax.broadcasted_iota(jnp.int32, (whole.shape[0], 128), 1)
    send[:, tail:] = jnp.where(
        lane == 0,
        high,
        jnp.where(lane == 1, middle, jnp.where(lane == 2, low, 0.0)),
    ).astype(bf16)


def act_body(total, got, out):
    hidden = out.shape[1]
    whole = total[...] + got[...].astype(f32)
    square = jnp.sum(whole[:, 2 * hidden :], axis=1, keepdims=True)
    inv_rms = lax.rsqrt(square / D + norm_eps)
    gate = whole[:, :hidden] * inv_rms
    up = whole[:, hidden : 2 * hidden] * inv_rms
    out[...] = (gate / (1.0 + jnp.exp(-gate)) * up).astype(bf16)


def down_one(act, w_down, expert):
    hid = w_down.shape[1]
    total = None
    for p in range(HSPLIT):
        part = dot(act[:, p * hid : (p + 1) * hid], w_down[expert * HSPLIT + p])
        total = part if total is None else total + part
    return total.astype(bf16)


def scatter_rows(away, own, core, shape):
    groups, packed, width = shape
    per = packed // 2
    lines = groups * CAP
    both = jnp.concatenate([away, own], axis=0)
    flat = jnp.concatenate([both[:, :width], both[:, width:]], axis=0)

    def want(row, col):
        half, block, line = col // (2 * lines), (col // lines) % 2, col % lines
        expert = jnp.where(block == 0, 1 - core, core)
        return row == (line // CAP) * packed + half * per + expert * CAP + line % CAP

    return dot(onehot((groups * packed, 4 * lines), want), flat)


def down_own_body(act, w_down, out):
    core = lax.axis_index("tp") % 2
    out[...] = down_one(act, w_down, core)


def down_away_body(act, w_down, done, out):
    core = lax.axis_index("tp") % 2
    away = down_one(act, w_down, 1 - core)
    table = scatter_rows(away, done[...], core, out.shape)
    out[...] = table.astype(bf16).reshape(out.shape)


def finish_body(state, back, mix, out):
    groups, packed, width = back.shape
    rows = state.shape[0]
    mixed = dot(mix[...], back[...].reshape(groups * packed, width))
    for half in range(2):
        base = half * 3 * rows
        add = (
            mixed[base : base + rows]
            + mixed[base + rows : base + 2 * rows]
            + mixed[base + 2 * rows : base + 3 * rows]
        )
        lanes = slice(half * width, (half + 1) * width)
        out[:, lanes] = (state[:, lanes].astype(f32) + add).astype(bf16)


def local(
    queries,
    cache,
    lengths,
    w_uv,
    w_out,
    residual,
    gain,
    expert_ids,
    expert_weights,
    w_gate,
    w_up,
    w_down,
):
    sec, ep, tp = (lax.axis_size(a) for a in ("sec", "ep", "tp"))
    axes = ("sec", "ep", "tp")
    rows, heads, _ = queries.shape
    columns = residual.shape[1]
    groups = sec * ep
    slots = EXPERTS // groups * CAP
    half = columns // 2
    hidden = HSPLIT * w_gate.shape[2]
    lines = groups * CAP
    packed = 2 * rows
    width = half + 128

    def swap(axis, bit):
        return [(i, i ^ bit) for i in range(lax.axis_size(axis))]

    def turn(flip):
        return [
            ((s * ep + e) * tp + t, ((s ^ flip) * ep + t) * tp + e)
            for s in range(sec)
            for e in range(ep)
            for t in range(tp)
        ]

    gain = gain.reshape(1, columns)
    (pick,) = call(start_body, [((4 * ep * rows, 4 * ep * rows), bf16)], (), [], cost=COSTS[0])
    (latent,) = call(
        latent_body,
        [((rows, heads, w_uv.shape[1]), f32)],
        (lengths, queries, cache, pick),
        [SMEM, VMEM, VMEM, VMEM],
        cost=COSTS[1],
    )
    (values,) = call(
        values_body,
        [((2 * packed, width), bf16)],
        (expert_ids, latent, w_uv, residual),
        [SMEM, VMEM, VMEM, VMEM],
        cost=COSTS[2],
    )
    blocks = [values] + [lax.ppermute(values, "ep", swap("ep", k)) for k in (1, 2, 3)]
    part, extra = call(
        project_body,
        [((ep * rows, columns), f32), ((2 * ep * rows, width), bf16)],
        (pick, *blocks, w_out),
        [VMEM] * 6,
        cost=COSTS[3],
    )
    got = lax.ppermute(part, "tp", swap("tp", 1))
    beyond = lax.ppermute(extra, "sec", swap("sec", 1))
    (part,) = call(add_body, [((ep * rows, columns), bf16)], (part, got), [VMEM] * 2, cost=COSTS[4])
    got = lax.ppermute(part, "tp", swap("tp", 2))
    (part,) = call(add_body, [((ep * rows, columns), bf16)], (part, got), [VMEM] * 2, cost=COSTS[5])
    same = lax.ppermute(part, axes, turn(0))
    cross = lax.ppermute(part, axes, turn(1))
    known, choice = call(
        choose_body,
        [((groups * rows, columns), f32), ((2 * lines + 8, groups * rows), bf16)],
        (extra, beyond),
        [VMEM] * 2,
    )
    (mix,) = call(
        mix_body, [((6 * rows, groups * 2 * slots), bf16)], (expert_ids, expert_weights), [SMEM] * 2
    )
    wide = 2 * hidden + 128
    away, mine, state = call(
        experts_away_body,
        [((lines, wide), f32), ((lines, columns), bf16), ((rows, columns), bf16)],
        (known, same, cross, choice, gain, w_gate, w_up),
        [VMEM] * 7,
        cost=COSTS[6],
    )
    away = lax.ppermute(away, "tp", swap("tp", 1))
    (own,) = call(
        experts_own_body,
        [((lines, wide), f32)],
        (mine, gain, w_gate, w_up),
        [VMEM] * 4,
        cost=COSTS[7],
    )
    total, send = call(
        merge_body, [((lines, wide), f32), ((lines, wide), bf16)], (own, away), [VMEM] * 2
    )
    got = lax.ppermute(send, "tp", swap("tp", 2))
    (act,) = call(act_body, [((lines, hidden), bf16)], (total, got), [VMEM] * 2)
    act_away = lax.ppermute(act, "tp", swap("tp", 1))
    (done,) = call(down_own_body, [((lines, columns), bf16)], (act, w_down), [VMEM] * 2)
    (back,) = call(
        down_away_body,
        [((groups, 2 * slots, half), bf16)],
        (act_away, w_down, done),
        [VMEM] * 3,
    )
    back = lax.all_to_all(back, ("sec", "ep"), split_axis=0, concat_axis=0, tiled=True)
    (out,) = call(finish_body, [((rows, columns), bf16)], (state, back, mix), [VMEM] * 3)
    return out


def local_any(
    queries,
    cache,
    lengths,
    w_uv,
    w_out,
    residual,
    gain,
    expert_ids,
    expert_weights,
    w_gate,
    w_up,
    w_down,
):
    req_rows = queries.shape[0]
    latent_width = w_uv.shape[1]
    scores = (
        jnp.einsum("rhc,rlc->rhl", queries, cache, preferred_element_type=jnp.float32) * score_scale
    )
    positions = lax.broadcasted_iota(jnp.int32, scores.shape, 2)
    live_mask = positions < lengths[:, None, None]
    scores = jnp.where(live_mask, scores, -1e30)
    row_top = jnp.max(scores, axis=-1, keepdims=True)
    raw_weights = jnp.where(live_mask, jnp.exp(scores - row_top), 0.0)
    probs = (raw_weights / jnp.sum(raw_weights, axis=-1, keepdims=True)).astype(jnp.bfloat16)
    latent = jnp.einsum(
        "rhl,rlc->rhc", probs, cache[:, :, :latent_width], preferred_element_type=jnp.float32
    ).astype(jnp.bfloat16)
    values = jnp.einsum("rhc,hcv->rhv", latent, w_uv, preferred_element_type=jnp.float32).astype(
        jnp.bfloat16
    )
    values = values.reshape(req_rows, -1)
    projected = jnp.dot(
        lax.all_gather(values, "ep", axis=0, tiled=True), w_out, preferred_element_type=jnp.float32
    )
    full_rows = lax.all_to_all(projected, "ep", split_axis=0, concat_axis=1, tiled=True)
    attention = lax.psum_scatter(full_rows, "tp", scatter_dimension=1, tiled=True)
    hidden_state = (residual.astype(jnp.float32) + attention).astype(jnp.bfloat16)
    column_count = hidden_state.shape[1]
    topk_count = expert_ids.shape[1]
    flat_ids = expert_ids.reshape(-1)
    onehot = (flat_ids[:, None] == jnp.arange(EXPERTS, dtype=jnp.int32)[None, :]).astype(jnp.int32)
    rank = jnp.sum((jnp.cumsum(onehot, axis=0) - onehot) * onehot, axis=1)
    slot_index = flat_ids * CAP + rank
    route_rows = jnp.repeat(hidden_state, topk_count, axis=0)
    slot_table = (
        jnp.zeros((EXPERTS * CAP, column_count), jnp.bfloat16).at[slot_index].set(route_rows)
    )
    sending = jnp.repeat(slot_table.reshape(EXPERTS, CAP, column_count), HSPLIT, axis=0)
    sec_count = lax.axis_size("sec")
    ep_count = lax.axis_size("ep")
    groups = sec_count * ep_count
    local_pieces = w_gate.shape[0]
    sending = sending.reshape(groups, local_pieces * CAP, column_count)
    received = lax.all_to_all(sending, ("sec", "ep"), split_axis=0, concat_axis=0, tiled=True)
    arrived = received.reshape(groups, local_pieces, CAP, column_count)
    arrived_wide = arrived.astype(jnp.float32)
    squares = jnp.sum(arrived_wide * arrived_wide, axis=-1)
    scaled = (arrived_wide * gain[None, None, None, :]).astype(jnp.bfloat16)
    gate_part = jnp.einsum("gpcd,pdh->gpch", scaled, w_gate, preferred_element_type=jnp.float32)
    up_part = jnp.einsum("gpcd,pdh->gpch", scaled, w_up, preferred_element_type=jnp.float32)
    gate_part, up_part, squares = lax.psum((gate_part, up_part, squares), "tp")
    inv_rms = lax.rsqrt(squares / D + norm_eps)[..., None]
    activated = (jax.nn.silu(gate_part * inv_rms) * (up_part * inv_rms)).astype(jnp.bfloat16)
    piece_out = jnp.einsum(
        "gpch,phd->gpcd", activated, w_down, preferred_element_type=jnp.float32
    ).astype(jnp.bfloat16)
    returned = lax.all_to_all(
        piece_out.reshape(groups, local_pieces * CAP, column_count),
        ("sec", "ep"),
        split_axis=0,
        concat_axis=0,
        tiled=True,
    )
    per_expert = jnp.sum(
        returned.reshape(EXPERTS, HSPLIT, CAP, column_count).astype(jnp.float32), axis=1
    )
    route_out = per_expert.reshape(EXPERTS * CAP, column_count)[slot_index]
    mixture = jnp.sum(
        route_out.reshape(req_rows, topk_count, column_count) * expert_weights[:, :, None], axis=1
    )
    return (hidden_state.astype(jnp.float32) + mixture).astype(jnp.bfloat16)


def solution(mesh):
    in_specs = (
        P(("sec", "ep"), "tp", None),
        P(("sec", "ep"), None, None),
        P(("sec", "ep")),
        P("tp", None, None),
        P("tp", "ep"),
        P(("sec", "ep"), "tp"),
        P("tp"),
        P(("sec", "ep"), None),
        P(("sec", "ep"), None),
        P(("sec", "ep"), "tp", None),
        P(("sec", "ep"), "tp", None),
        P(("sec", "ep"), None, "tp"),
    )
    out_specs = P(("sec", "ep"), "tp")
    shape = mesh.shape
    small = shape["ep"] == 4 and shape["tp"] == 4 and shape["sec"] == 2
    body = local if small else local_any
    return jax.shard_map(body, mesh=mesh, in_specs=in_specs, out_specs=out_specs, check_vma=False)
```

```python
import functools

import jax
import jax.numpy as jnp
from jax import lax
from jax.experimental import pallas as pl
from jax.experimental.pallas import tpu as pltpu
from jax.sharding import PartitionSpec as P

D = 7168
HSPLIT = 8
EXPERTS = 16
CAP = 2


score_scale = 0.07216878364870322
norm_eps = 1e-06

f32 = jnp.float32
bf16 = jnp.bfloat16
VMEM = pl.BlockSpec(memory_space=pltpu.VMEM)
SMEM = pl.BlockSpec(memory_space=pltpu.SMEM)


def cost(micros):
    return pl.CostEstimate(flops=micros * 1_000_000_000, bytes_accessed=1_000_000, transcendentals=0)


COSTS = [cost(m) for m in (20, 1, 20, 60, 1, 1, 20, 20)]


def call(body, outs, args, specs, scratch=(), limit=4 << 20, cost=None):
    return pl.pallas_call(
        body,
        out_shape=[jax.ShapeDtypeStruct(s, d) for s, d in outs],
        in_specs=specs,
        out_specs=[VMEM] * len(outs),
        scratch_shapes=list(scratch),
        compiler_params=pltpu.CompilerParams(vmem_limit_bytes=limit),
        cost_estimate=cost,
    )(*args)


def dot(a, b):
    return jnp.dot(a, b, preferred_element_type=f32)


def onehot(shape, want):
    row = lax.broadcasted_iota(jnp.int32, shape, 0)
    col = lax.broadcasted_iota(jnp.int32, shape, 1)
    return want(row, col).astype(f32).astype(bf16)


def start_body(pick):
    me = lax.axis_index("ep")
    lines = pick.shape[0]
    block = lines // 4
    rows = block // 4

    def want(row, col):
        kind, e, r = row // block, (row % block) // rows, row % rows
        return col == (e ^ me) * block + kind * rows + r

    pick[...] = onehot(pick.shape, want)


def latent_body(lengths, queries, cache, pick, latent):
    rows, heads, _ = queries.shape
    width = latent.shape[2]
    scores = jnp.concatenate(
        [
            lax.dot_general(
                queries[r], cache[r], (((1,), (1,)), ((), ())), preferred_element_type=f32
            )
            for r in range(rows)
        ],
        axis=0,
    )
    owner = lax.broadcasted_iota(jnp.int32, scores.shape, 0) // heads
    limit = jnp.full(scores.shape, lengths[0], jnp.int32)
    for r in range(1, rows):
        limit = jnp.where(owner == r, lengths[r], limit)
    live = lax.broadcasted_iota(jnp.int32, scores.shape, 1) < limit
    scores = jnp.where(live, scores * score_scale, -1e30)
    top = jnp.max(scores, axis=-1, keepdims=True)
    raw = jnp.where(live, jnp.exp(scores - top), 0.0)
    probs = (raw / jnp.sum(raw, axis=-1, keepdims=True)).astype(bf16)
    for r in range(rows):
        latent[r] = dot(probs[r * heads : (r + 1) * heads], cache[r, :, :width])


def values_body(ids, latent, w_uv, residual, out):
    rows, heads, _ = latent.shape
    per = heads // 2
    halves = []
    for piece in range(2):
        parts = [
            dot(latent[:, h, :].astype(bf16), w_uv[h]) for h in range(piece * per, (piece + 1) * per)
        ]
        halves.append(jnp.concatenate(parts, axis=1))
    packed = 2 * rows
    out[:packed] = jnp.concatenate(halves, axis=0).astype(bf16)
    span = residual.shape[1] // 2
    wide = residual[...].astype(f32)
    row = lax.broadcasted_iota(jnp.int32, (rows, 128), 0)
    lane = lax.broadcasted_iota(jnp.int32, (rows, 128), 1)
    named = jnp.zeros((rows, 128), f32)
    for r in range(rows):
        for k in range(ids.shape[1]):
            named = jnp.where((row == r) & (lane == k), ids[r, k].astype(f32), named)
    halves = [
        jnp.concatenate([wide[:, h * span : (h + 1) * span], named], axis=1) for h in range(2)
    ]
    out[packed:] = jnp.concatenate(halves, axis=0).astype(bf16)


def project_body(pick, own, got1, got2, got3, w_out, out, extra):
    packed = own.shape[0] // 2
    flat = jnp.concatenate([ref[...] for ref in (own, got1, got2, got3)], axis=0)
    block, width = out.shape[0], own.shape[1]
    table = dot(pick[...], flat).astype(bf16)
    out[...] = dot(table[:block], w_out[:width]) + dot(table[block : 2 * block], w_out[width:])
    extra[...] = table[2 * block :]


def add_body(one, two, out):
    out[...] = (one[...].astype(f32) + two[...].astype(f32)).astype(bf16)


def choose_body(extra, got, known, choice):
    me, sec = lax.axis_index("ep"), lax.axis_index("sec")
    block = extra.shape[0] // 2
    rows = block // 4
    tokens = 2 * block
    span = known.shape[1] // 2
    first = jnp.concatenate([extra[:block], got[:block]], axis=0)
    second = jnp.concatenate([extra[block:], got[block:]], axis=0)
    known[:, :span] = first[:, :span].astype(f32)
    known[:, span:] = second[:, :span].astype(f32)
    ids = first[:, span:].astype(f32)
    lane = lax.broadcasted_iota(jnp.int32, ids.shape, 1)
    hits = jnp.zeros(ids.shape, f32)
    local_experts = EXPERTS // (2 * 4)
    for x in range(local_experts):
        expert = ((sec * 4 + me) * local_experts + x).astype(f32)
        found = jnp.sum(jnp.where((lane < 4) & (ids == expert), 1.0, 0.0), axis=1, keepdims=True)
        hits = hits + jnp.where(lane == x, found, 0.0)
    hits = hits.astype(bf16)
    across = lax.dot_general(
        onehot((8, 128), lambda row, col: row == col),
        hits,
        (((1,), (1,)), ((), ())),
        preferred_element_type=f32,
    )
    earlier = dot(
        across.astype(bf16),
        onehot((tokens, tokens), lambda row, col: (row // rows == col // rows) & (row < col)),
    )
    slots = 2 * 4 * CAP
    row = lax.broadcasted_iota(jnp.int32, (slots, tokens), 0)
    col = lax.broadcasted_iota(jnp.int32, (slots, tokens), 1)
    group, rank = row // CAP, (row % CAP).astype(f32)
    same = (group % 4 == (col % block) // rows) & ((group // 4) ^ sec == col // block)
    for x in range(local_experts):
        hit = jnp.broadcast_to(across[x : x + 1], (slots, tokens))
        before = jnp.broadcast_to(earlier[x : x + 1], (slots, tokens))
        choice[x * slots : (x + 1) * slots] = jnp.where(
            same & (hit > 0.5) & (before == rank), 1.0, 0.0
        ).astype(bf16)
    choice[local_experts * slots :] = onehot(
        (8, tokens), lambda row, col: (row < rows) & (col == me * rows + row)
    )


def mix_body(ids, weights, mix):
    rows, top = ids.shape
    slots = []
    for r in range(rows):
        for k in range(top):
            expert = ids[r, k]
            rank = jnp.int32(0)
            for q in range(r):
                for j in range(top):
                    rank = rank + (ids[q, j] == expert).astype(jnp.int32)
            slots.append((r, k, expert * CAP + rank))
    packed = 8
    per = packed // 2
    row = lax.broadcasted_iota(jnp.int32, mix.shape, 0)
    col = lax.broadcasted_iota(jnp.int32, mix.shape, 1)
    slot = (col // packed) * per + col % per
    half = (col % packed) // per
    acc = jnp.zeros(mix.shape, f32)
    for r, k, where in slots:
        acc = acc + jnp.where(
            (slot == where) & (row // (3 * rows) == half) & (row % rows == r), weights[r, k], 0.0
        )
    high = acc.astype(bf16)
    left = acc - high.astype(f32)
    middle = left.astype(bf16)
    low = (left - middle.astype(f32)).astype(bf16)
    part = (row // rows) % 3
    mix[...] = jnp.where(
        part == 0, high.astype(f32), jnp.where(part == 1, middle.astype(f32), low.astype(f32))
    ).astype(bf16)


def three_terms(square):
    high = square.astype(bf16).astype(f32)
    middle = (square - high).astype(bf16).astype(f32)
    low = square - high - middle
    lane = lax.broadcasted_iota(jnp.int32, (square.shape[0], 128), 1)
    return jnp.where(
        lane == 0, high, jnp.where(lane == 1, middle, jnp.where(lane == 2, low, 0.0))
    )


def expert_partial(rows, gain, w_gate, w_up, expert, part, out):
    scaled = (rows * gain[...]).astype(bf16)
    hid = w_gate.shape[2]
    count = HSPLIT // 2
    for p in range(count):
        at = expert * HSPLIT + part * count + p
        out[:, p * hid : (p + 1) * hid] = dot(scaled, w_gate[at])
        out[:, (count + p) * hid : (count + p + 1) * hid] = dot(scaled, w_up[at])
    if part == 0:
        out[:, 2 * count * hid :] = three_terms(jnp.sum(rows * rows, axis=1, keepdims=True))


def experts_away_body(known, same, other, choice, gain, w_gate, w_up, out0, out1, mine, state):
    core = lax.axis_index("tp") % 2
    block = same.shape[0]
    lines = out0.shape[0]
    hidden = jnp.concatenate(
        [
            (known[:block] + same[...].astype(f32)).astype(bf16),
            (known[block:] + other[...].astype(f32)).astype(bf16),
        ],
        axis=0,
    )
    table = dot(choice[...], hidden)
    first, second = table[:lines], table[lines : 2 * lines]
    mine[...] = jnp.where(core == 0, first, second).astype(bf16)
    state[...] = table[2 * lines : 2 * lines + state.shape[0]].astype(bf16)

    rows = jnp.where(core == 0, second, first)
    expert_partial(rows, gain, w_gate, w_up, 1 - core, 0, out0)
    expert_partial(rows, gain, w_gate, w_up, 1 - core, 1, out1)


def experts_own_body(part, mine, gain, w_gate, w_up, out):
    core = lax.axis_index("tp") % 2
    expert_partial(mine[...].astype(f32), gain, w_gate, w_up, core, part, out)


def merge_body(tail, own, got, total, send):
    whole = own[...] + got[...]
    total[...] = whole
    send[:, :tail] = whole[:, :tail].astype(bf16)
    if whole.shape[1] > tail:
        square = jnp.sum(whole[:, tail:], axis=1, keepdims=True)
        send[:, tail:] = three_terms(square).astype(bf16)


def act_body(total0, got0, total1, got1, out):
    part = out.shape[1] // 2
    inv_rms = None
    for i, (total, got) in enumerate(((total0, got0), (total1, got1))):
        whole = total[...] + got[...].astype(f32)
        if i == 0:
            square = jnp.sum(whole[:, 2 * part :], axis=1, keepdims=True)
            inv_rms = lax.rsqrt(square / D + norm_eps)
        gate = whole[:, :part] * inv_rms
        up = whole[:, part : 2 * part] * inv_rms
        out[:, i * part : (i + 1) * part] = (gate / (1.0 + jnp.exp(-gate)) * up).astype(bf16)


def down_one(act, w_down, expert):
    hid = w_down.shape[1]
    total = None
    for p in range(HSPLIT):
        part = dot(act[:, p * hid : (p + 1) * hid], w_down[expert * HSPLIT + p])
        total = part if total is None else total + part
    return total.astype(bf16)


def scatter_rows(away, own, core, shape):
    groups, packed, width = shape
    per = packed // 2
    lines = groups * CAP
    both = jnp.concatenate([away, own], axis=0)
    flat = jnp.concatenate([both[:, :width], both[:, width:]], axis=0)

    def want(row, col):
        half, block, line = col // (2 * lines), (col // lines) % 2, col % lines
        expert = jnp.where(block == 0, 1 - core, core)
        return row == (line // CAP) * packed + half * per + expert * CAP + line % CAP

    return dot(onehot((groups * packed, 4 * lines), want), flat)


def down_own_body(act, w_down, out):
    core = lax.axis_index("tp") % 2
    out[...] = down_one(act, w_down, core)


def down_away_body(act, w_down, done, out):
    core = lax.axis_index("tp") % 2
    away = down_one(act, w_down, 1 - core)
    table = scatter_rows(away, done[...], core, out.shape)
    out[...] = table.astype(bf16).reshape(out.shape)


def finish_body(state, back, mix, out):
    groups, packed, width = back.shape
    rows = state.shape[0]
    mixed = dot(mix[...], back[...].reshape(groups * packed, width))
    for half in range(2):
        base = half * 3 * rows
        add = (
            mixed[base : base + rows]
            + mixed[base + rows : base + 2 * rows]
            + mixed[base + 2 * rows : base + 3 * rows]
        )
        lanes = slice(half * width, (half + 1) * width)
        out[:, lanes] = (state[:, lanes].astype(f32) + add).astype(bf16)


def local(
    queries,
    cache,
    lengths,
    w_uv,
    w_out,
    residual,
    gain,
    expert_ids,
    expert_weights,
    w_gate,
    w_up,
    w_down,
):
    sec, ep, tp = (lax.axis_size(a) for a in ("sec", "ep", "tp"))
    axes = ("sec", "ep", "tp")
    rows, heads, _ = queries.shape
    columns = residual.shape[1]
    groups = sec * ep
    slots = EXPERTS // groups * CAP
    half = columns // 2
    hidden = HSPLIT * w_gate.shape[2]
    lines = groups * CAP
    packed = 2 * rows
    width = half + 128

    def swap(axis, bit):
        return [(i, i ^ bit) for i in range(lax.axis_size(axis))]

    def turn(flip):
        return [
            ((s * ep + e) * tp + t, ((s ^ flip) * ep + t) * tp + e)
            for s in range(sec)
            for e in range(ep)
            for t in range(tp)
        ]

    gain = gain.reshape(1, columns)
    (pick,) = call(start_body, [((4 * ep * rows, 4 * ep * rows), bf16)], (), [], cost=COSTS[0])
    (latent,) = call(
        latent_body,
        [((rows, heads, w_uv.shape[1]), f32)],
        (lengths, queries, cache, pick),
        [SMEM, VMEM, VMEM, VMEM],
        cost=COSTS[1],
    )
    (values,) = call(
        values_body,
        [((2 * packed, width), bf16)],
        (expert_ids, latent, w_uv, residual),
        [SMEM, VMEM, VMEM, VMEM],
        cost=COSTS[2],
    )
    blocks = [values] + [lax.ppermute(values, "ep", swap("ep", k)) for k in (1, 2, 3)]
    part, extra = call(
        project_body,
        [((ep * rows, columns), f32), ((2 * ep * rows, width), bf16)],
        (pick, *blocks, w_out),
        [VMEM] * 6,
        cost=COSTS[3],
    )
    got = lax.ppermute(part, "tp", swap("tp", 1))
    beyond = lax.ppermute(extra, "sec", swap("sec", 1))
    (part,) = call(add_body, [((ep * rows, columns), bf16)], (part, got), [VMEM] * 2, cost=COSTS[4])
    got = lax.ppermute(part, "tp", swap("tp", 2))
    (part,) = call(add_body, [((ep * rows, columns), bf16)], (part, got), [VMEM] * 2, cost=COSTS[5])
    same = lax.ppermute(part, axes, turn(0))
    cross = lax.ppermute(part, axes, turn(1))
    known, choice = call(
        choose_body,
        [((groups * rows, columns), f32), ((2 * lines + 8, groups * rows), bf16)],
        (extra, beyond),
        [VMEM] * 2,
    )
    (mix,) = call(
        mix_body, [((6 * rows, groups * 2 * slots), bf16)], (expert_ids, expert_weights), [SMEM] * 2
    )
    wides = (hidden + 128, hidden)
    away0, away1, mine, state = call(
        experts_away_body,
        [((lines, w), f32) for w in wides] + [((lines, columns), bf16), ((rows, columns), bf16)],
        (known, same, cross, choice, gain, w_gate, w_up),
        [VMEM] * 7,
        cost=COSTS[6],
    )
    done = []
    for i, away in enumerate((away0, away1)):
        away = lax.ppermute(away, "tp", swap("tp", 1))
        (own,) = call(
            functools.partial(experts_own_body, i),
            [((lines, wides[i]), f32)],
            (mine, gain, w_gate, w_up),
            [VMEM] * 4,
            cost=COSTS[7],
        )
        total, send = call(
            functools.partial(merge_body, hidden),
            [((lines, wides[i]), f32), ((lines, wides[i]), bf16)],
            (own, away),
            [VMEM] * 2,
        )
        done += [total, lax.ppermute(send, "tp", swap("tp", 2))]
    (act,) = call(act_body, [((lines, hidden), bf16)], tuple(done), [VMEM] * 4)
    act_away = lax.ppermute(act, "tp", swap("tp", 1))
    (done,) = call(down_own_body, [((lines, columns), bf16)], (act, w_down), [VMEM] * 2)
    (back,) = call(
        down_away_body,
        [((groups, 2 * slots, half), bf16)],
        (act_away, w_down, done),
        [VMEM] * 3,
    )
    back = lax.all_to_all(back, ("sec", "ep"), split_axis=0, concat_axis=0, tiled=True)
    (out,) = call(finish_body, [((rows, columns), bf16)], (state, back, mix), [VMEM] * 3)
    return out


def local_any(
    queries,
    cache,
    lengths,
    w_uv,
    w_out,
    residual,
    gain,
    expert_ids,
    expert_weights,
    w_gate,
    w_up,
    w_down,
):
    req_rows = queries.shape[0]
    latent_width = w_uv.shape[1]
    scores = (
        jnp.einsum("rhc,rlc->rhl", queries, cache, preferred_element_type=jnp.float32) * score_scale
    )
    positions = lax.broadcasted_iota(jnp.int32, scores.shape, 2)
    live_mask = positions < lengths[:, None, None]
    scores = jnp.where(live_mask, scores, -1e30)
    row_top = jnp.max(scores, axis=-1, keepdims=True)
    raw_weights = jnp.where(live_mask, jnp.exp(scores - row_top), 0.0)
    probs = (raw_weights / jnp.sum(raw_weights, axis=-1, keepdims=True)).astype(jnp.bfloat16)
    latent = jnp.einsum(
        "rhl,rlc->rhc", probs, cache[:, :, :latent_width], preferred_element_type=jnp.float32
    ).astype(jnp.bfloat16)
    values = jnp.einsum("rhc,hcv->rhv", latent, w_uv, preferred_element_type=jnp.float32).astype(
        jnp.bfloat16
    )
    values = values.reshape(req_rows, -1)
    projected = jnp.dot(
        lax.all_gather(values, "ep", axis=0, tiled=True), w_out, preferred_element_type=jnp.float32
    )
    full_rows = lax.all_to_all(projected, "ep", split_axis=0, concat_axis=1, tiled=True)
    attention = lax.psum_scatter(full_rows, "tp", scatter_dimension=1, tiled=True)
    hidden_state = (residual.astype(jnp.float32) + attention).astype(jnp.bfloat16)
    column_count = hidden_state.shape[1]
    topk_count = expert_ids.shape[1]
    flat_ids = expert_ids.reshape(-1)
    onehot = (flat_ids[:, None] == jnp.arange(EXPERTS, dtype=jnp.int32)[None, :]).astype(jnp.int32)
    rank = jnp.sum((jnp.cumsum(onehot, axis=0) - onehot) * onehot, axis=1)
    slot_index = flat_ids * CAP + rank
    route_rows = jnp.repeat(hidden_state, topk_count, axis=0)
    slot_table = (
        jnp.zeros((EXPERTS * CAP, column_count), jnp.bfloat16).at[slot_index].set(route_rows)
    )
    sending = jnp.repeat(slot_table.reshape(EXPERTS, CAP, column_count), HSPLIT, axis=0)
    sec_count = lax.axis_size("sec")
    ep_count = lax.axis_size("ep")
    groups = sec_count * ep_count
    local_pieces = w_gate.shape[0]
    sending = sending.reshape(groups, local_pieces * CAP, column_count)
    received = lax.all_to_all(sending, ("sec", "ep"), split_axis=0, concat_axis=0, tiled=True)
    arrived = received.reshape(groups, local_pieces, CAP, column_count)
    arrived_wide = arrived.astype(jnp.float32)
    squares = jnp.sum(arrived_wide * arrived_wide, axis=-1)
    scaled = (arrived_wide * gain[None, None, None, :]).astype(jnp.bfloat16)
    gate_part = jnp.einsum("gpcd,pdh->gpch", scaled, w_gate, preferred_element_type=jnp.float32)
    up_part = jnp.einsum("gpcd,pdh->gpch", scaled, w_up, preferred_element_type=jnp.float32)
    gate_part, up_part, squares = lax.psum((gate_part, up_part, squares), "tp")
    inv_rms = lax.rsqrt(squares / D + norm_eps)[..., None]
    activated = (jax.nn.silu(gate_part * inv_rms) * (up_part * inv_rms)).astype(jnp.bfloat16)
    piece_out = jnp.einsum(
        "gpch,phd->gpcd", activated, w_down, preferred_element_type=jnp.float32
    ).astype(jnp.bfloat16)
    returned = lax.all_to_all(
        piece_out.reshape(groups, local_pieces * CAP, column_count),
        ("sec", "ep"),
        split_axis=0,
        concat_axis=0,
        tiled=True,
    )
    per_expert = jnp.sum(
        returned.reshape(EXPERTS, HSPLIT, CAP, column_count).astype(jnp.float32), axis=1
    )
    route_out = per_expert.reshape(EXPERTS * CAP, column_count)[slot_index]
    mixture = jnp.sum(
        route_out.reshape(req_rows, topk_count, column_count) * expert_weights[:, :, None], axis=1
    )
    return (hidden_state.astype(jnp.float32) + mixture).astype(jnp.bfloat16)


def solution(mesh):
    in_specs = (
        P(("sec", "ep"), "tp", None),
        P(("sec", "ep"), None, None),
        P(("sec", "ep")),
        P("tp", None, None),
        P("tp", "ep"),
        P(("sec", "ep"), "tp"),
        P("tp"),
        P(("sec", "ep"), None),
        P(("sec", "ep"), None),
        P(("sec", "ep"), "tp", None),
        P(("sec", "ep"), "tp", None),
        P(("sec", "ep"), None, "tp"),
    )
    out_specs = P(("sec", "ep"), "tp")
    shape = mesh.shape
    small = shape["ep"] == 4 and shape["tp"] == 4 and shape["sec"] == 2
    body = local if small else local_any
    return jax.shard_map(body, mesh=mesh, in_specs=in_specs, out_specs=out_specs, check_vma=False)
```

```python
import functools

import jax
import jax.numpy as jnp
from jax import lax
from jax.experimental import pallas as pl
from jax.experimental.pallas import tpu as pltpu
from jax.sharding import PartitionSpec as P

D = 7168
HSPLIT = 8
EXPERTS = 16
CAP = 2


score_scale = 0.07216878364870322
norm_eps = 1e-06

f32 = jnp.float32
bf16 = jnp.bfloat16
VMEM = pl.BlockSpec(memory_space=pltpu.VMEM)
SMEM = pl.BlockSpec(memory_space=pltpu.SMEM)


def cost(micros):
    return pl.CostEstimate(flops=micros * 1_000_000_000, bytes_accessed=1_000_000, transcendentals=0)


COSTS = [cost(m) for m in (20, 1, 20, 60, 1, 1, 20, 20)]


def call(body, outs, args, specs, scratch=(), limit=4 << 20, cost=None):
    return pl.pallas_call(
        body,
        out_shape=[jax.ShapeDtypeStruct(s, d) for s, d in outs],
        in_specs=specs,
        out_specs=[VMEM] * len(outs),
        scratch_shapes=list(scratch),
        compiler_params=pltpu.CompilerParams(vmem_limit_bytes=limit),
        cost_estimate=cost,
    )(*args)


def dot(a, b):
    return jnp.dot(a, b, preferred_element_type=f32)


def onehot(shape, want):
    row = lax.broadcasted_iota(jnp.int32, shape, 0)
    col = lax.broadcasted_iota(jnp.int32, shape, 1)
    return want(row, col).astype(f32).astype(bf16)


def start_body(pick):
    me = lax.axis_index("ep")
    lines = pick.shape[0]
    block = lines // 4
    rows = block // 4

    def want(row, col):
        kind, e, r = row // block, (row % block) // rows, row % rows
        return col == (e ^ me) * block + kind * rows + r

    pick[...] = onehot(pick.shape, want)


def latent_body(lengths, queries, cache, pick, latent):
    rows, heads, _ = queries.shape
    width = latent.shape[2]
    scores = jnp.concatenate(
        [
            lax.dot_general(
                queries[r], cache[r], (((1,), (1,)), ((), ())), preferred_element_type=f32
            )
            for r in range(rows)
        ],
        axis=0,
    )
    owner = lax.broadcasted_iota(jnp.int32, scores.shape, 0) // heads
    limit = jnp.full(scores.shape, lengths[0], jnp.int32)
    for r in range(1, rows):
        limit = jnp.where(owner == r, lengths[r], limit)
    live = lax.broadcasted_iota(jnp.int32, scores.shape, 1) < limit
    scores = jnp.where(live, scores * score_scale, -1e30)
    top = jnp.max(scores, axis=-1, keepdims=True)
    raw = jnp.where(live, jnp.exp(scores - top), 0.0)
    probs = (raw / jnp.sum(raw, axis=-1, keepdims=True)).astype(bf16)
    for r in range(rows):
        latent[r] = dot(probs[r * heads : (r + 1) * heads], cache[r, :, :width])


def values_body(ids, latent, w_uv, residual, out):
    rows, heads, _ = latent.shape
    per = heads // 2
    halves = []
    for piece in range(2):
        parts = [
            dot(latent[:, h, :].astype(bf16), w_uv[h]) for h in range(piece * per, (piece + 1) * per)
        ]
        halves.append(jnp.concatenate(parts, axis=1))
    packed = 2 * rows
    out[:packed] = jnp.concatenate(halves, axis=0).astype(bf16)
    span = residual.shape[1] // 2
    wide = residual[...].astype(f32)
    row = lax.broadcasted_iota(jnp.int32, (rows, 128), 0)
    lane = lax.broadcasted_iota(jnp.int32, (rows, 128), 1)
    named = jnp.zeros((rows, 128), f32)
    for r in range(rows):
        for k in range(ids.shape[1]):
            named = jnp.where((row == r) & (lane == k), ids[r, k].astype(f32), named)
    halves = [
        jnp.concatenate([wide[:, h * span : (h + 1) * span], named], axis=1) for h in range(2)
    ]
    out[packed:] = jnp.concatenate(halves, axis=0).astype(bf16)


def project_body(pick, own, got1, got2, got3, w_out, out, extra):
    packed = own.shape[0] // 2
    flat = jnp.concatenate([ref[...] for ref in (own, got1, got2, got3)], axis=0)
    block, width = out.shape[0], own.shape[1]
    table = dot(pick[...], flat).astype(bf16)
    out[...] = dot(table[:block], w_out[:width]) + dot(table[block : 2 * block], w_out[width:])
    extra[...] = table[2 * block :]


def add_body(one, two, out):
    out[...] = (one[...].astype(f32) + two[...].astype(f32)).astype(bf16)


def choose_body(extra, got, ids, weights, known, choice, mix):
    write_mix(ids, weights, mix)
    me, sec = lax.axis_index("ep"), lax.axis_index("sec")
    block = extra.shape[0] // 2
    rows = block // 4
    tokens = 2 * block
    span = known.shape[1] // 2
    first = jnp.concatenate([extra[:block], got[:block]], axis=0)
    second = jnp.concatenate([extra[block:], got[block:]], axis=0)
    known[:, :span] = first[:, :span].astype(f32)
    known[:, span:] = second[:, :span].astype(f32)
    ids = first[:, span:].astype(f32)
    lane = lax.broadcasted_iota(jnp.int32, ids.shape, 1)
    hits = jnp.zeros(ids.shape, f32)
    local_experts = EXPERTS // (2 * 4)
    for x in range(local_experts):
        expert = ((sec * 4 + me) * local_experts + x).astype(f32)
        found = jnp.sum(jnp.where((lane < 4) & (ids == expert), 1.0, 0.0), axis=1, keepdims=True)
        hits = hits + jnp.where(lane == x, found, 0.0)
    hits = hits.astype(bf16)
    across = lax.dot_general(
        onehot((8, 128), lambda row, col: row == col),
        hits,
        (((1,), (1,)), ((), ())),
        preferred_element_type=f32,
    )
    earlier = dot(
        across.astype(bf16),
        onehot((tokens, tokens), lambda row, col: (row // rows == col // rows) & (row < col)),
    )
    slots = 2 * 4 * CAP
    row = lax.broadcasted_iota(jnp.int32, (slots, tokens), 0)
    col = lax.broadcasted_iota(jnp.int32, (slots, tokens), 1)
    group, rank = row // CAP, (row % CAP).astype(f32)
    same = (group % 4 == (col % block) // rows) & ((group // 4) ^ sec == col // block)
    for x in range(local_experts):
        hit = jnp.broadcast_to(across[x : x + 1], (slots, tokens))
        before = jnp.broadcast_to(earlier[x : x + 1], (slots, tokens))
        choice[x * slots : (x + 1) * slots] = jnp.where(
            same & (hit > 0.5) & (before == rank), 1.0, 0.0
        ).astype(bf16)
    choice[local_experts * slots :] = onehot(
        (8, tokens), lambda row, col: (row < rows) & (col == me * rows + row)
    )


def write_mix(ids, weights, mix):
    rows, top = ids.shape
    slots = []
    for r in range(rows):
        for k in range(top):
            expert = ids[r, k]
            rank = jnp.int32(0)
            for q in range(r):
                for j in range(top):
                    rank = rank + (ids[q, j] == expert).astype(jnp.int32)
            slots.append((r, k, expert * CAP + rank))
    packed = 8
    per = packed // 2
    row = lax.broadcasted_iota(jnp.int32, mix.shape, 0)
    col = lax.broadcasted_iota(jnp.int32, mix.shape, 1)
    slot = (col // packed) * per + col % per
    half = (col % packed) // per
    acc = jnp.zeros(mix.shape, f32)
    for r, k, where in slots:
        acc = acc + jnp.where(
            (slot == where) & (row // (3 * rows) == half) & (row % rows == r), weights[r, k], 0.0
        )
    high = acc.astype(bf16)
    left = acc - high.astype(f32)
    middle = left.astype(bf16)
    low = (left - middle.astype(f32)).astype(bf16)
    part = (row // rows) % 3
    mix[...] = jnp.where(
        part == 0, high.astype(f32), jnp.where(part == 1, middle.astype(f32), low.astype(f32))
    ).astype(bf16)


def three_terms(square):
    high = square.astype(bf16).astype(f32)
    middle = (square - high).astype(bf16).astype(f32)
    low = square - high - middle
    lane = lax.broadcasted_iota(jnp.int32, (square.shape[0], 128), 1)
    return jnp.where(
        lane == 0, high, jnp.where(lane == 1, middle, jnp.where(lane == 2, low, 0.0))
    )


def expert_partial(rows, gain, w_gate, w_up, expert, part, out):
    scaled = (rows * gain[...]).astype(bf16)
    hid = w_gate.shape[2]
    count = HSPLIT // 2
    for p in range(count):
        at = expert * HSPLIT + part * count + p
        out[:, p * hid : (p + 1) * hid] = dot(scaled, w_gate[at])
        out[:, (count + p) * hid : (count + p + 1) * hid] = dot(scaled, w_up[at])
    if part == 0:
        out[:, 2 * count * hid :] = three_terms(jnp.sum(rows * rows, axis=1, keepdims=True))


def experts_away_body(known, same, other, choice, gain, w_gate, w_up, out0, out1, mine, state):
    core = lax.axis_index("tp") % 2
    block = same.shape[0]
    lines = out0.shape[0]
    hidden = jnp.concatenate(
        [
            (known[:block] + same[...].astype(f32)).astype(bf16),
            (known[block:] + other[...].astype(f32)).astype(bf16),
        ],
        axis=0,
    )
    table = dot(choice[...], hidden)
    first, second = table[:lines], table[lines : 2 * lines]
    mine[...] = jnp.where(core == 0, first, second).astype(bf16)
    state[...] = table[2 * lines : 2 * lines + state.shape[0]].astype(bf16)

    rows = jnp.where(core == 0, second, first)
    expert_partial(rows, gain, w_gate, w_up, 1 - core, 0, out0)
    expert_partial(rows, gain, w_gate, w_up, 1 - core, 1, out1)


def experts_own_body(part, mine, gain, w_gate, w_up, out):
    core = lax.axis_index("tp") % 2
    expert_partial(mine[...].astype(f32), gain, w_gate, w_up, core, part, out)


def merge_body(tail, own, got, total, send):
    whole = own[...] + got[...]
    total[...] = whole
    send[:, :tail] = whole[:, :tail].astype(bf16)
    if whole.shape[1] > tail:
        square = jnp.sum(whole[:, tail:], axis=1, keepdims=True)
        send[:, tail:] = three_terms(square).astype(bf16)


def act_body(total0, got0, total1, got1, out):
    part = out.shape[1] // 2
    inv_rms = None
    for i, (total, got) in enumerate(((total0, got0), (total1, got1))):
        whole = total[...] + got[...].astype(f32)
        if i == 0:
            square = jnp.sum(whole[:, 2 * part :], axis=1, keepdims=True)
            inv_rms = lax.rsqrt(square / D + norm_eps)
        gate = whole[:, :part] * inv_rms
        up = whole[:, part : 2 * part] * inv_rms
        out[:, i * part : (i + 1) * part] = (gate / (1.0 + jnp.exp(-gate)) * up).astype(bf16)


def down_one(act, w_down, expert):
    hid = w_down.shape[1]
    total = None
    for p in range(HSPLIT):
        part = dot(act[:, p * hid : (p + 1) * hid], w_down[expert * HSPLIT + p])
        total = part if total is None else total + part
    return total.astype(bf16)


def scatter_rows(away, own, core, shape):
    groups, packed, width = shape
    per = packed // 2
    lines = groups * CAP
    both = jnp.concatenate([away, own], axis=0)
    flat = jnp.concatenate([both[:, :width], both[:, width:]], axis=0)

    def want(row, col):
        half, block, line = col // (2 * lines), (col // lines) % 2, col % lines
        expert = jnp.where(block == 0, 1 - core, core)
        return row == (line // CAP) * packed + half * per + expert * CAP + line % CAP

    return dot(onehot((groups * packed, 4 * lines), want), flat)


def down_own_body(act, w_down, out):
    core = lax.axis_index("tp") % 2
    out[...] = down_one(act, w_down, core)


def down_away_body(act, w_down, done, out):
    core = lax.axis_index("tp") % 2
    away = down_one(act, w_down, 1 - core)
    table = scatter_rows(away, done[...], core, out.shape)
    out[...] = table.astype(bf16).reshape(out.shape)


def finish_body(state, back, mix, out):
    groups, packed, width = back.shape
    rows = state.shape[0]
    mixed = dot(mix[...], back[...].reshape(groups * packed, width))
    for half in range(2):
        base = half * 3 * rows
        add = (
            mixed[base : base + rows]
            + mixed[base + rows : base + 2 * rows]
            + mixed[base + 2 * rows : base + 3 * rows]
        )
        lanes = slice(half * width, (half + 1) * width)
        out[:, lanes] = (state[:, lanes].astype(f32) + add).astype(bf16)


def local(
    queries,
    cache,
    lengths,
    w_uv,
    w_out,
    residual,
    gain,
    expert_ids,
    expert_weights,
    w_gate,
    w_up,
    w_down,
):
    sec, ep, tp = (lax.axis_size(a) for a in ("sec", "ep", "tp"))
    axes = ("sec", "ep", "tp")
    rows, heads, _ = queries.shape
    columns = residual.shape[1]
    groups = sec * ep
    slots = EXPERTS // groups * CAP
    half = columns // 2
    hidden = HSPLIT * w_gate.shape[2]
    lines = groups * CAP
    packed = 2 * rows
    width = half + 128

    def swap(axis, bit):
        return [(i, i ^ bit) for i in range(lax.axis_size(axis))]

    def turn(flip):
        return [
            ((s * ep + e) * tp + t, ((s ^ flip) * ep + t) * tp + e)
            for s in range(sec)
            for e in range(ep)
            for t in range(tp)
        ]

    gain = gain.reshape(1, columns)
    (pick,) = call(start_body, [((4 * ep * rows, 4 * ep * rows), bf16)], (), [], cost=COSTS[0])
    (latent,) = call(
        latent_body,
        [((rows, heads, w_uv.shape[1]), f32)],
        (lengths, queries, cache, pick),
        [SMEM, VMEM, VMEM, VMEM],
        cost=COSTS[1],
    )
    (values,) = call(
        values_body,
        [((2 * packed, width), bf16)],
        (expert_ids, latent, w_uv, residual),
        [SMEM, VMEM, VMEM, VMEM],
        cost=COSTS[2],
    )
    blocks = [values] + [lax.ppermute(values, "ep", swap("ep", k)) for k in (1, 2, 3)]
    part, extra = call(
        project_body,
        [((ep * rows, columns), f32), ((2 * ep * rows, width), bf16)],
        (pick, *blocks, w_out),
        [VMEM] * 6,
        cost=COSTS[3],
    )
    got = lax.ppermute(part, "tp", swap("tp", 1))
    beyond = lax.ppermute(extra, "sec", swap("sec", 1))
    (part,) = call(add_body, [((ep * rows, columns), bf16)], (part, got), [VMEM] * 2, cost=COSTS[4])
    got = lax.ppermute(part, "tp", swap("tp", 2))
    (part,) = call(add_body, [((ep * rows, columns), bf16)], (part, got), [VMEM] * 2, cost=COSTS[5])
    same = lax.ppermute(part, axes, turn(0))
    cross = lax.ppermute(part, axes, turn(1))
    known, choice, mix = call(
        choose_body,
        [
            ((groups * rows, columns), f32),
            ((2 * lines + 8, groups * rows), bf16),
            ((6 * rows, groups * 2 * slots), bf16),
        ],
        (extra, beyond, expert_ids, expert_weights),
        [VMEM, VMEM, SMEM, SMEM],
    )
    wides = (hidden + 128, hidden)
    away0, away1, mine, state = call(
        experts_away_body,
        [((lines, w), f32) for w in wides] + [((lines, columns), bf16), ((rows, columns), bf16)],
        (known, same, cross, choice, gain, w_gate, w_up),
        [VMEM] * 7,
        cost=COSTS[6],
    )
    done = []
    for i, away in enumerate((away0, away1)):
        away = lax.ppermute(away, "tp", swap("tp", 1))
        (own,) = call(
            functools.partial(experts_own_body, i),
            [((lines, wides[i]), f32)],
            (mine, gain, w_gate, w_up),
            [VMEM] * 4,
            cost=COSTS[7],
        )
        total, send = call(
            functools.partial(merge_body, hidden),
            [((lines, wides[i]), f32), ((lines, wides[i]), bf16)],
            (own, away),
            [VMEM] * 2,
        )
        done += [total, lax.ppermute(send, "tp", swap("tp", 2))]
    (act,) = call(act_body, [((lines, hidden), bf16)], tuple(done), [VMEM] * 4)
    act_away = lax.ppermute(act, "tp", swap("tp", 1))
    (done,) = call(down_own_body, [((lines, columns), bf16)], (act, w_down), [VMEM] * 2)
    (back,) = call(
        down_away_body,
        [((groups, 2 * slots, half), bf16)],
        (act_away, w_down, done),
        [VMEM] * 3,
    )
    back = lax.all_to_all(back, ("sec", "ep"), split_axis=0, concat_axis=0, tiled=True)
    (out,) = call(finish_body, [((rows, columns), bf16)], (state, back, mix), [VMEM] * 3)
    return out


def local_any(
    queries,
    cache,
    lengths,
    w_uv,
    w_out,
    residual,
    gain,
    expert_ids,
    expert_weights,
    w_gate,
    w_up,
    w_down,
):
    req_rows = queries.shape[0]
    latent_width = w_uv.shape[1]
    scores = (
        jnp.einsum("rhc,rlc->rhl", queries, cache, preferred_element_type=jnp.float32) * score_scale
    )
    positions = lax.broadcasted_iota(jnp.int32, scores.shape, 2)
    live_mask = positions < lengths[:, None, None]
    scores = jnp.where(live_mask, scores, -1e30)
    row_top = jnp.max(scores, axis=-1, keepdims=True)
    raw_weights = jnp.where(live_mask, jnp.exp(scores - row_top), 0.0)
    probs = (raw_weights / jnp.sum(raw_weights, axis=-1, keepdims=True)).astype(jnp.bfloat16)
    latent = jnp.einsum(
        "rhl,rlc->rhc", probs, cache[:, :, :latent_width], preferred_element_type=jnp.float32
    ).astype(jnp.bfloat16)
    values = jnp.einsum("rhc,hcv->rhv", latent, w_uv, preferred_element_type=jnp.float32).astype(
        jnp.bfloat16
    )
    values = values.reshape(req_rows, -1)
    projected = jnp.dot(
        lax.all_gather(values, "ep", axis=0, tiled=True), w_out, preferred_element_type=jnp.float32
    )
    full_rows = lax.all_to_all(projected, "ep", split_axis=0, concat_axis=1, tiled=True)
    attention = lax.psum_scatter(full_rows, "tp", scatter_dimension=1, tiled=True)
    hidden_state = (residual.astype(jnp.float32) + attention).astype(jnp.bfloat16)
    column_count = hidden_state.shape[1]
    topk_count = expert_ids.shape[1]
    flat_ids = expert_ids.reshape(-1)
    onehot = (flat_ids[:, None] == jnp.arange(EXPERTS, dtype=jnp.int32)[None, :]).astype(jnp.int32)
    rank = jnp.sum((jnp.cumsum(onehot, axis=0) - onehot) * onehot, axis=1)
    slot_index = flat_ids * CAP + rank
    route_rows = jnp.repeat(hidden_state, topk_count, axis=0)
    slot_table = (
        jnp.zeros((EXPERTS * CAP, column_count), jnp.bfloat16).at[slot_index].set(route_rows)
    )
    sending = jnp.repeat(slot_table.reshape(EXPERTS, CAP, column_count), HSPLIT, axis=0)
    sec_count = lax.axis_size("sec")
    ep_count = lax.axis_size("ep")
    groups = sec_count * ep_count
    local_pieces = w_gate.shape[0]
    sending = sending.reshape(groups, local_pieces * CAP, column_count)
    received = lax.all_to_all(sending, ("sec", "ep"), split_axis=0, concat_axis=0, tiled=True)
    arrived = received.reshape(groups, local_pieces, CAP, column_count)
    arrived_wide = arrived.astype(jnp.float32)
    squares = jnp.sum(arrived_wide * arrived_wide, axis=-1)
    scaled = (arrived_wide * gain[None, None, None, :]).astype(jnp.bfloat16)
    gate_part = jnp.einsum("gpcd,pdh->gpch", scaled, w_gate, preferred_element_type=jnp.float32)
    up_part = jnp.einsum("gpcd,pdh->gpch", scaled, w_up, preferred_element_type=jnp.float32)
    gate_part, up_part, squares = lax.psum((gate_part, up_part, squares), "tp")
    inv_rms = lax.rsqrt(squares / D + norm_eps)[..., None]
    activated = (jax.nn.silu(gate_part * inv_rms) * (up_part * inv_rms)).astype(jnp.bfloat16)
    piece_out = jnp.einsum(
        "gpch,phd->gpcd", activated, w_down, preferred_element_type=jnp.float32
    ).astype(jnp.bfloat16)
    returned = lax.all_to_all(
        piece_out.reshape(groups, local_pieces * CAP, column_count),
        ("sec", "ep"),
        split_axis=0,
        concat_axis=0,
        tiled=True,
    )
    per_expert = jnp.sum(
        returned.reshape(EXPERTS, HSPLIT, CAP, column_count).astype(jnp.float32), axis=1
    )
    route_out = per_expert.reshape(EXPERTS * CAP, column_count)[slot_index]
    mixture = jnp.sum(
        route_out.reshape(req_rows, topk_count, column_count) * expert_weights[:, :, None], axis=1
    )
    return (hidden_state.astype(jnp.float32) + mixture).astype(jnp.bfloat16)


def solution(mesh):
    in_specs = (
        P(("sec", "ep"), "tp", None),
        P(("sec", "ep"), None, None),
        P(("sec", "ep")),
        P("tp", None, None),
        P("tp", "ep"),
        P(("sec", "ep"), "tp"),
        P("tp"),
        P(("sec", "ep"), None),
        P(("sec", "ep"), None),
        P(("sec", "ep"), "tp", None),
        P(("sec", "ep"), "tp", None),
        P(("sec", "ep"), None, "tp"),
    )
    out_specs = P(("sec", "ep"), "tp")
    shape = mesh.shape
    small = shape["ep"] == 4 and shape["tp"] == 4 and shape["sec"] == 2
    body = local if small else local_any
    return jax.shard_map(body, mesh=mesh, in_specs=in_specs, out_specs=out_specs, check_vma=False)
```
